32 devices in a mesh: fsdp: 32 (over z, y, x, core).
Axes of the slice: x: 2, y: 2, z: 4, core: 2. Of those that a mesh axis runs over, the one named last changes fastest.
Arguments:
- hidden_in: bfloat16 [16384, 1024], P('fsdp'), may hold values from -6 to 6
- out_grad: bfloat16 [16384, 1024], P('fsdp'), may hold values from -6 to 6
- segment_ids: int32 [64, 256], P('fsdp'), may hold values from 0 to 3, never falling along the last dimension, each value on 1 to 128 neighbouring positions
- norm_gains: float32 [2, 1024], P(None, 'fsdp'), may hold values from 0.5 to 1.5
- bias_rows: float32 [6, 1024], P(None, 'fsdp'), may hold values from -3 to 3
- heads_weight: float32 [1024, 3072], P('fsdp'), may hold values from -0.1875 to 0.1875
- output_weight: float32 [1024, 1024], P('fsdp'), may hold values from -0.75 to 0.75
- expand_weight: float32 [1024, 4096], P('fsdp'), may hold values from -0.1875 to 0.1875
- widen_bias: float32 [4096], P('fsdp'), may hold values from -3 to 3
- shrink_weight: float32 [4096, 1024], P('fsdp'), may hold values from -0.09375 to 0.09375
- moment_gains: float32 [2, 1024], P(None, 'fsdp'), may hold values from -80 to 80
- moment_biases: float32 [6, 1024], P(None, 'fsdp'), may hold values from -80 to 80
- moment_heads: float32 [1024, 3072], P('fsdp'), may hold values from -24 to 24
- moment_output: float32 [1024, 1024], P('fsdp'), may hold values from -24 to 24
- moment_expand: float32 [1024, 4096], P('fsdp'), may hold values from -24 to 24
- moment_widen: float32 [4096], P('fsdp'), may hold values from -24 to 24
- moment_shrink: float32 [4096, 1024], P('fsdp'), may hold values from -24 to 24
- square_gains: float32 [2, 1024], P(None, 'fsdp'), may hold values from 327.68 to 3276.8
- square_biases: float32 [6, 1024], P(None, 'fsdp'), may hold values from 327.68 to 3276.8
- square_heads: float32 [1024, 3072], P('fsdp'), may hold values from 32.768 to 327.68
- square_output: float32 [1024, 1024], P('fsdp'), may hold values from 32.768 to 327.68
- square_expand: float32 [1024, 4096], P('fsdp'), may hold values from 32.768 to 327.68
- square_widen: float32 [4096], P('fsdp'), may hold values from 32.768 to 327.68
- square_shrink: float32 [4096, 1024], P('fsdp'), may hold values from 32.768 to 327.68
Outputs:
- block_out: bfloat16 [16384, 1024], P('fsdp')
- input_gradient: float32 [16384, 1024], P('fsdp')
- gradient_gains: float32 [2, 1024], P(None, 'fsdp')
- gradient_biases: float32 [6, 1024], P(None, 'fsdp')
- gradient_heads: float32 [1024, 3072], P('fsdp')
- gradient_output: float32 [1024, 1024], P('fsdp')
- gradient_expand: float32 [1024, 4096], P('fsdp')
- gradient_widen: float32 [4096], P('fsdp')
- gradient_shrink: float32 [4096, 1024], P('fsdp')
- updated_gains: float32 [2, 1024], P(None, 'fsdp')
- updated_biases: float32 [6, 1024], P(None, 'fsdp')
- updated_heads: float32 [1024, 3072], P('fsdp')
- updated_output: float32 [1024, 1024], P('fsdp')
- updated_expand: float32 [1024, 4096], P('fsdp')
- updated_widen: float32 [4096], P('fsdp')
- updated_shrink: float32 [4096, 1024], P('fsdp')
- momentum_gains: float32 [2, 1024], P(None, 'fsdp')
- momentum_biases: float32 [6, 1024], P(None, 'fsdp')
- momentum_heads: float32 [1024, 3072], P('fsdp')
- momentum_output: float32 [1024, 1024], P('fsdp')
- momentum_expand: float32 [1024, 4096], P('fsdp')
- momentum_widen: float32 [4096], P('fsdp')
- momentum_shrink: float32 [4096, 1024], P('fsdp')
- variance_gains: float32 [2, 1024], P(None, 'fsdp')
- variance_biases: float32 [6, 1024], P(None, 'fsdp')
- variance_heads: float32 [1024, 3072], P('fsdp')
- variance_output: float32 [1024, 1024], P('fsdp')
- variance_expand: float32 [1024, 4096], P('fsdp')
- variance_widen: float32 [4096], P('fsdp')
- variance_shrink: float32 [4096, 1024], P('fsdp')
The draws below stay inside these ranges and needn't reach their ends.
Inputs may be any that keep to these rules, and one draw needn't show every extreme that they name: `segment_ids`: ids never fall along a row; a document has at most 128 tokens, and some document of every row has exactly that many.
All inputs are finite; a program needn't handle non-finite values.
Results may differ from the reference program's by a relative error of at most 0.0085.
The reference program's roundings to bfloat16 on the way count: a program that leaves them out, or rounds other values in their place, can miss the bound.
Values may be sent and summed in bfloat16 or wider, within the bound.
No kernel may reach another device: no remote copies, remote signals or barrier semaphores. Data moves between devices by JAX's collectives and lax.ppermute only.
A program may use at most 192 MiB of HBM per device.

```python
import math
import jax
import jax.numpy as jnp
import numpy as np
from jax import lax

D = 1024
FF = 4096
HEAD_DIM = 64
LEN = 256
ADAM_STEP = 3
SEQS = 64
TOKENS = 16384


def level_of(own_key, extent, cuts, low, top_value):
    level, own = 1.0, jax.random.fold_in(own_key, 6)
    for position, blocks in cuts:
        heights = jnp.exp(jax.random.uniform(jax.random.fold_in(own, position), (blocks,), jnp.float32, low / len(cuts), top_value / len(cuts)))
        level = level * jnp.repeat(heights, extent[position] // blocks).reshape([-1 if axis == position else 1 for axis in range(len(extent))])
    return level


def profile(count, total, bound, lean):
    portions = [(1 << 20) // math.isqrt(rank ** lean) + 1 for rank in range(2, count + 1)]
    surplus, holding = total - bound - (count - 1), [1] * (count - 1)
    while surplus > 0:
        candidates = [i for i in range(count - 1) if holding[i] < bound]
        whole, remaining = sum([portions[i] for i in candidates]), surplus
        for i in candidates:
            addition = min(bound - holding[i], max(1, remaining * portions[i] // whole), surplus)
            holding[i] = holding[i] + addition
            surplus = surplus - addition
    return np.array([bound] + holding)


def uneven_parts(own_key, amount, total, most, skew):
    if amount == 2:
        one = jax.random.randint(own_key, (), max(1, total - most), min(most, total - 1) + 1)
        return jnp.stack([one, total - one])
    lengths = jnp.asarray(profile(amount, total, most, skew), jnp.int32)
    couples = (amount - 1) // 2
    source_of, receiver = lengths[1:1 + 2 * couples:2], lengths[2:2 + 2 * couples:2]
    margin = jnp.minimum(source_of - 1, most - receiver)
    shifted = jax.random.randint(jax.random.fold_in(own_key, 1), (couples,), 0, 1 << 20) % (margin + 1)
    lengths = lengths.at[1:1 + 2 * couples:2].set(source_of - shifted).at[2:2 + 2 * couples:2].set(receiver + shifted)
    return lengths[jax.random.permutation(jax.random.fold_in(own_key, 2), amount)]


def gaussian(own_key, dims, scale, limit, cuts=(), kind=jnp.bfloat16):
    factor_of = level_of(own_key, dims, cuts, -0.22, 0.18) if cuts else 1.0
    drawn = jax.random.normal(own_key, dims, jnp.float32) * scale * factor_of
    return jnp.minimum(jnp.maximum(drawn, -limit), limit).astype(kind)


def setup_inputs(seed: int = 0) -> dict:
    key_list = jax.random.split(jax.random.key(seed), 25)
    hidden_in = gaussian(key_list[0], (TOKENS, D), 1.0, 6.0, ((0, 32),))
    out_grad = gaussian(key_list[1], (TOKENS, D), 1.0, 6.0, ((0, 32),))
    segment_ids = jax.vmap(lambda own: jnp.searchsorted(jnp.cumsum(uneven_parts(own, 4, LEN, LEN // 2, 0)), jnp.arange(LEN), side="right"))(jax.random.split(key_list[2], SEQS)).reshape((SEQS, LEN)).astype(jnp.int32)
    norm_gains = jnp.clip(1.0 + 0.1 * jax.random.normal(key_list[3], (2, D), jnp.float32), 0.5, 1.5)
    bias_rows = gaussian(key_list[4], (6, D), 0.5, 3.0, ((1, 32),), jnp.float32)
    heads_weight = gaussian(key_list[5], (D, 3 * D), D ** -0.5, 0.1875, ((0, 32),), jnp.float32)
    output_weight = gaussian(key_list[6], (D, D), (D // 16) ** -0.5, 0.75, ((0, 32),), jnp.float32)
    expand_weight = gaussian(key_list[7], (D, FF), D ** -0.5, 0.1875, ((0, 32),), jnp.float32)
    widen_bias = gaussian(key_list[8], (FF,), 0.5, 3.0, ((0, 32),), jnp.float32)
    shrink_weight = gaussian(key_list[9], (FF, D), FF ** -0.5, 0.09375, ((0, 32),), jnp.float32)
    moment_gains = gaussian(key_list[10], (2, D), (0.1 * TOKENS ** 0.5), 80.0, ((1, 32),), jnp.float32)
    moment_biases = gaussian(key_list[11], (6, D), (0.1 * TOKENS ** 0.5), 80.0, ((1, 32),), jnp.float32)
    moment_heads = gaussian(key_list[12], (D, 3 * D), (0.03 * TOKENS ** 0.5), 24.0, ((0, 32),), jnp.float32)
    moment_output = gaussian(key_list[13], (D, D), (0.03 * TOKENS ** 0.5), 24.0, ((0, 32),), jnp.float32)
    moment_expand = gaussian(key_list[14], (D, FF), (0.03 * TOKENS ** 0.5), 24.0, ((0, 32),), jnp.float32)
    moment_widen = gaussian(key_list[15], (FF,), (0.03 * TOKENS ** 0.5), 24.0, ((0, 32),), jnp.float32)
    moment_shrink = gaussian(key_list[16], (FF, D), (0.03 * TOKENS ** 0.5), 24.0, ((0, 32),), jnp.float32)
    square_gains = jnp.clip(jnp.exp(math.log(3276.8) - 2.3025851 * jax.random.uniform(key_list[17], (2, D), jnp.float32) ** level_of(key_list[17], (2, D), ((1, 32),), -0.2, 0.2)), 327.68, 3276.8)
    square_biases = jnp.clip(jnp.exp(math.log(3276.8) - 2.3025851 * jax.random.uniform(key_list[18], (6, D), jnp.float32) ** level_of(key_list[18], (6, D), ((1, 32),), -0.2, 0.2)), 327.68, 3276.8)
    square_heads = jnp.clip(jnp.exp(math.log(327.68) - 2.30258502 * jax.random.uniform(key_list[19], (D, 3 * D), jnp.float32) ** level_of(key_list[19], (D, 3 * D), ((0, 32),), -0.2, 0.2)), 32.768, 327.68)
    square_output = jnp.clip(jnp.exp(math.log(327.68) - 2.30258502 * jax.random.uniform(key_list[20], (D, D), jnp.float32) ** level_of(key_list[20], (D, D), ((0, 32),), -0.2, 0.2)), 32.768, 327.68)
    square_expand = jnp.clip(jnp.exp(math.log(327.68) - 2.30258502 * jax.random.uniform(key_list[21], (D, FF), jnp.float32) ** level_of(key_list[21], (D, FF), ((0, 32),), -0.2, 0.2)), 32.768, 327.68)
    square_widen = jnp.clip(jnp.exp(math.log(327.68) - 2.30258502 * jax.random.uniform(key_list[22], (FF,), jnp.float32) ** level_of(key_list[22], (FF,), ((0, 32),), -0.2, 0.2)), 32.768, 327.68)
    square_shrink = jnp.clip(jnp.exp(math.log(327.68) - 2.30258502 * jax.random.uniform(key_list[23], (FF, D), jnp.float32) ** level_of(key_list[23], (FF, D), ((0, 32),), -0.2, 0.2)), 32.768, 327.68)
    return dict(hidden_in=hidden_in, out_grad=out_grad, segment_ids=segment_ids, norm_gains=norm_gains, bias_rows=bias_rows, heads_weight=heads_weight, output_weight=output_weight, expand_weight=expand_weight, widen_bias=widen_bias, shrink_weight=shrink_weight, moment_gains=moment_gains, moment_biases=moment_biases, moment_heads=moment_heads, moment_output=moment_output, moment_expand=moment_expand, moment_widen=moment_widen, moment_shrink=moment_shrink, square_gains=square_gains, square_biases=square_biases, square_heads=square_heads, square_output=square_output, square_expand=square_expand, square_widen=square_widen, square_shrink=square_shrink)


EPS_NORM = 1e-05
GELU_C = 0.7978845608
GELU_A = 0.044715
LEARN_RATES = (0.4, 0.4, 0.02, 0.02, 0.02, 0.4, 0.02)
DECAYS = (0.0, 0.0, 0.1, 0.1, 0.1, 0.0, 0.1)

def layer_norm_apply(value_rows):
    centred = value_rows - lax.optimization_barrier(jnp.mean(value_rows, -1, keepdims=True))
    spread = lax.optimization_barrier(jnp.mean(centred * centred, -1, keepdims=True))
    factor = lax.rsqrt(spread + EPS_NORM)
    return (centred * factor, factor)

def norm_backward_pass(scaled, normed, factor):
    first = lax.optimization_barrier(jnp.mean(scaled, -1, keepdims=True))
    second = lax.optimization_barrier(jnp.mean(scaled * normed, -1, keepdims=True))
    return factor * (scaled - first - normed * second)

def gelu_tanh(upper_projection):
    inner = GELU_C * (upper_projection + GELU_A * upper_projection * upper_projection * upper_projection)
    return 0.5 * upper_projection * (1.0 + jnp.tanh(inner))

def gelu_slope(upper_projection):
    inner = GELU_C * (upper_projection + GELU_A * upper_projection * upper_projection * upper_projection)
    tangent = jnp.tanh(inner)
    return 0.5 * (1.0 + tangent) + 0.5 * upper_projection * (1.0 - tangent * tangent) * GELU_C * (1.0 + 3.0 * GELU_A * upper_projection * upper_projection)

def inner_rows(left, right):
    return lax.dot_general(left, right, (((0,), (0,)), ((), ())), preferred_element_type=jnp.float32)

def outer_cols(left, right):
    return lax.dot_general(left, right, (((1,), (1,)), ((), ())), preferred_element_type=jnp.float32)

def score_terms(query_rows, key_rows, segs):
    length = query_rows.shape[0]
    heads = query_rows.shape[1] // HEAD_DIM
    q_three = query_rows.reshape(length, heads, HEAD_DIM).astype(jnp.float32)
    k_three = key_rows.reshape(length, heads, HEAD_DIM).astype(jnp.float32)
    places = jnp.arange(length, dtype=jnp.int32)
    distance = (places[:, None] - places[None, :]).astype(jnp.float32)
    allowed = (places[:, None] >= places[None, :]) & (segs[:, None] == segs[None, :])
    slopes = 2.0 ** (-8.0 * (jnp.arange(heads, dtype=jnp.float32) + 1.0) / heads)
    scores = jnp.einsum('ihd,jhd->hij', q_three, k_three) * HEAD_DIM ** (-0.5) - slopes[:, None, None] * distance[None]
    return jnp.where(allowed[None], scores, -1e+30)

def attend(query_rows, key_rows, value_rows, segs):
    length, width = query_rows.shape
    heads = width // HEAD_DIM
    scores = score_terms(query_rows, key_rows, segs)
    log_sum_exponent = jnp.log(lax.optimization_barrier(jnp.sum(jnp.exp(scores), -1)))
    probs = jnp.exp(scores - log_sum_exponent[..., None]).astype(jnp.bfloat16)
    v_three = value_rows.reshape(length, heads, HEAD_DIM).astype(jnp.float32)
    attended_rows = jnp.einsum('hij,jhd->ihd', probs.astype(jnp.float32), v_three)
    return (attended_rows.reshape(length, width).astype(jnp.bfloat16), log_sum_exponent)

def attend_back(query_rows, key_rows, value_rows, attended_rows, log_sum_exponent, d_attended, segs):
    length, width = query_rows.shape
    heads = width // HEAD_DIM
    scores = score_terms(query_rows, key_rows, segs)
    probs = jnp.exp(scores - log_sum_exponent[..., None])
    probs_half = probs.astype(jnp.bfloat16).astype(jnp.float32)
    d_three = d_attended.reshape(length, heads, HEAD_DIM).astype(jnp.float32)
    a_three = attended_rows.reshape(length, heads, HEAD_DIM).astype(jnp.float32)
    delta = lax.optimization_barrier(jnp.sum(d_three * a_three, -1)).T
    v_three = value_rows.reshape(length, heads, HEAD_DIM).astype(jnp.float32)
    d_values = jnp.einsum('hij,ihd->jhd', probs_half, d_three)
    d_probs = jnp.einsum('ihd,jhd->hij', d_three, v_three)
    d_scores = (probs * (d_probs - delta[..., None]) * HEAD_DIM ** (-0.5)).astype(jnp.bfloat16).astype(jnp.float32)
    q_three = query_rows.reshape(length, heads, HEAD_DIM).astype(jnp.float32)
    k_three = key_rows.reshape(length, heads, HEAD_DIM).astype(jnp.float32)
    d_query = jnp.einsum('hij,jhd->ihd', d_scores, k_three)
    d_keys = jnp.einsum('hij,ihd->jhd', d_scores, q_three)
    return (d_query.reshape(length, width), d_keys.reshape(length, width), d_values.reshape(length, width))

def forward(params, hidden, segs):
    gains, biases, heads_w, output_w, expand_w, widen_b, shrink_w = params
    gain_float = gains.astype(jnp.float32)
    bias_float = biases.astype(jnp.float32)
    width = hidden.shape[1]
    start_offset = hidden.astype(jnp.float32)
    first_centred_scaled, first_factor = layer_norm_apply(start_offset)
    first_normed = (first_centred_scaled * gain_float[0] + bias_float[0]).astype(jnp.bfloat16)
    mixed = jnp.dot(first_normed, heads_w, preferred_element_type=jnp.float32)
    query_rows = (mixed[:, :width] + bias_float[1]).astype(jnp.bfloat16)
    key_rows = mixed[:, width:2 * width].astype(jnp.bfloat16)
    value_rows = (mixed[:, 2 * width:] + bias_float[2]).astype(jnp.bfloat16)
    attended_rows, log_sum_exponent = attend(query_rows, key_rows, value_rows, segs)
    first_hidden = start_offset + jnp.dot(attended_rows, output_w, preferred_element_type=jnp.float32) + bias_float[3]
    second_centred_scaled, second_factor = layer_norm_apply(first_hidden)
    second_normed = (second_centred_scaled * gain_float[1] + bias_float[4]).astype(jnp.bfloat16)
    upper_projection = jnp.dot(second_normed, expand_w, preferred_element_type=jnp.float32) + widen_b.astype(jnp.float32)
    active_units = gelu_tanh(upper_projection).astype(jnp.bfloat16)
    result = first_hidden + jnp.dot(active_units, shrink_w, preferred_element_type=jnp.float32) + bias_float[5]
    saved_residuals = (first_centred_scaled, first_factor, first_normed, query_rows, key_rows, value_rows, attended_rows, log_sum_exponent, second_centred_scaled, second_factor, second_normed, upper_projection, active_units)
    return (result.astype(jnp.bfloat16), saved_residuals)

def backward(params, saved_residuals, out_grad, segs):
    gains, biases, heads_w, output_w, expand_w, widen_b, shrink_w = params
    first_centred_scaled, first_factor, first_normed, query_rows, key_rows, value_rows, attended_rows, log_sum_exponent, second_centred_scaled, second_factor, second_normed, upper_projection, active_units = saved_residuals
    gain_float = gains.astype(jnp.float32)
    output_gradient = out_grad.astype(jnp.float32)
    g_shrink_bias = lax.optimization_barrier(jnp.sum(output_gradient, 0))
    g_shrink = inner_rows(active_units, out_grad)
    d_upper = outer_cols(out_grad, shrink_w) * gelu_slope(upper_projection)
    d_upper_half = d_upper.astype(jnp.bfloat16)
    g_widen = lax.optimization_barrier(jnp.sum(d_upper, 0))
    g_expand = inner_rows(second_normed, d_upper_half)
    second_normed_gradient = outer_cols(d_upper_half, expand_w)
    second_gain_gradient = lax.optimization_barrier(jnp.sum(second_normed_gradient * second_centred_scaled, 0))
    g_bias_two = lax.optimization_barrier(jnp.sum(second_normed_gradient, 0))
    hidden_gradient = output_gradient + norm_backward_pass(second_normed_gradient * gain_float[1], second_centred_scaled, second_factor)
    d_hidden_half = hidden_gradient.astype(jnp.bfloat16)
    g_output_bias = lax.optimization_barrier(jnp.sum(hidden_gradient, 0))
    g_output = inner_rows(attended_rows, d_hidden_half)
    d_attended = outer_cols(d_hidden_half, output_w).astype(jnp.bfloat16)
    d_query, d_keys, d_values = attend_back(query_rows, key_rows, value_rows, attended_rows, log_sum_exponent, d_attended, segs)
    g_query_bias = lax.optimization_barrier(jnp.sum(d_query, 0))
    g_value_bias = lax.optimization_barrier(jnp.sum(d_values, 0))
    d_mixed = jnp.concatenate([d_query, d_keys, d_values], 1).astype(jnp.bfloat16)
    g_heads = inner_rows(first_normed, d_mixed)
    first_normed_gradient = outer_cols(d_mixed, heads_w)
    first_gain_gradient = lax.optimization_barrier(jnp.sum(first_normed_gradient * first_centred_scaled, 0))
    g_bias_one = lax.optimization_barrier(jnp.sum(first_normed_gradient, 0))
    input_grad_rows = hidden_gradient + norm_backward_pass(first_normed_gradient * gain_float[0], first_centred_scaled, first_factor)
    g_gains = jnp.stack([first_gain_gradient, second_gain_gradient])
    g_biases = jnp.stack([g_bias_one, g_query_bias, g_value_bias, g_output_bias, g_bias_two, g_shrink_bias])
    return (input_grad_rows, (g_gains, g_biases, g_heads, g_output, g_expand, g_widen, g_shrink))

def adamw(weight, grad, moment, square, decay, rate):
    moment_next = 0.9 * moment + 0.1 * grad
    square_next = 0.95 * square + 0.05 * grad * grad
    first = moment_next / (1.0 - 0.9 ** ADAM_STEP)
    second = square_next / (1.0 - 0.95 ** ADAM_STEP)
    change = first / (jnp.sqrt(second) + 1e-08) + decay * weight
    return (weight - rate * change, moment_next, square_next)

def reference(hidden_in, out_grad, segment_ids, norm_gains, bias_rows, heads_weight, output_weight, expand_weight, widen_bias, shrink_weight, moment_gains, moment_biases, moment_heads, moment_output, moment_expand, moment_widen, moment_shrink, square_gains, square_biases, square_heads, square_output, square_expand, square_widen, square_shrink):
    masters = (norm_gains, bias_rows, heads_weight, output_weight, expand_weight, widen_bias, shrink_weight)
    moments = (moment_gains, moment_biases, moment_heads, moment_output, moment_expand, moment_widen, moment_shrink)
    squares = (square_gains, square_biases, square_heads, square_output, square_expand, square_widen, square_shrink)
    params = tuple((item.astype(jnp.bfloat16) for item in masters))
    count, length = segment_ids.shape
    width = hidden_in.shape[1]
    inputs = hidden_in.reshape(count, length, width)
    cotangents = out_grad.reshape(count, length, width)

    def one_sequence(totals, pieces):
        hidden, grad_out, segs = pieces
        result, saved_residuals = forward(params, hidden, segs)
        input_grad_rows, grads = backward(params, saved_residuals, grad_out, segs)
        totals = tuple((left + right for left, right in zip(totals, grads)))
        return (totals, (result, input_grad_rows))
    start_offset = tuple((jnp.zeros(item.shape, jnp.float32) for item in masters))
    totals, (results, d_inputs) = lax.scan(one_sequence, start_offset, (inputs, cotangents, segment_ids))
    updated = []
    momenta = []
    variances = []
    for weight, grad, moment, square, decay, rate in zip(masters, totals, moments, squares, DECAYS, LEARN_RATES):
        fresh, moment_next, square_next = adamw(weight, grad, moment, square, decay, rate)
        updated.append(fresh)
        momenta.append(moment_next)
        variances.append(square_next)
    return (results.reshape(count * length, width), d_inputs.reshape(count * length, width), totals[0], totals[1], totals[2], totals[3], totals[4], totals[5], totals[6], updated[0], updated[1], updated[2], updated[3], updated[4], updated[5], updated[6], momenta[0], momenta[1], momenta[2], momenta[3], momenta[4], momenta[5], momenta[6], variances[0], variances[1], variances[2], variances[3], variances[4], variances[5], variances[6])
```

```python
import jax
import jax.numpy as jnp
from jax import lax
from jax.experimental import pallas as pl
from jax.experimental.pallas import tpu as pltpu
from jax.sharding import PartitionSpec as P

HEAD_DIM = 64
ADAM_STEP = 3

AXIS = "fsdp"
EPS_NORM = 1e-05
GELU_C = 0.7978845608
GELU_A = 0.044715
LEARN_RATES = (0.4, 0.4, 0.02, 0.02, 0.02, 0.4, 0.02)
DECAYS = (0.0, 0.0, 0.1, 0.1, 0.1, 0.0, 0.1)


CORE, PAIR_X, PAIR_Y = 1, 2, 4


def swap(value, offset, count):
    return lax.ppermute(value, AXIS, [(i, i ^ offset) for i in range(count)])


def after(value, *tokens):
    return lax.optimization_barrier((value, *tokens))[0]


def line_bits(count):
    bits, bit = [], count // 2
    while bit > PAIR_Y:
        bits.append(bit)
        bit //= 2
    return bits


def gather_line(shard, count, *tokens):
    stack, offsets = after(shard, *tokens)[None], [0]
    for bit in line_bits(count):
        stack = jnp.concatenate([stack, swap(stack, bit, count)], 0)
        offsets = offsets + [o ^ bit for o in offsets]
    return stack, offsets


def gather_pair(stack, offsets, count, *tokens):
    stack = after(stack, *tokens)
    half = len(offsets) // 2
    by_y = swap(stack, PAIR_Y, count)
    by_x = swap(stack, PAIR_X, count)
    low = swap(by_y[:half], PAIR_X, count)
    high = swap(by_x[half:], PAIR_Y, count)
    both = PAIR_X ^ PAIR_Y
    return [
        (stack, offsets),
        (by_y, [o ^ PAIR_Y for o in offsets]),
        (by_x, [o ^ PAIR_X for o in offsets]),
        (low, [o ^ both for o in offsets[:half]]),
        (high, [o ^ both for o in offsets[half:]]),
    ]


def gather_core(pieces, count):
    return pieces + [(swap(b, CORE, count), [o ^ CORE for o in offs]) for b, offs in pieces]


def assemble(pieces, count, cuts):
    rows = pieces[0][0].shape[1]
    dtype = pieces[0][0].dtype
    width = cuts[-1]
    spans = list(zip(cuts[:-1], cuts[1:]))
    where = [(k, q, off) for k, (_, offs) in enumerate(pieces) for q, off in enumerate(offs)]

    def kernel(*refs):
        inputs, outputs = refs[: len(pieces)], refs[len(pieces) : len(pieces) + len(spans)]
        held, sem_in, sem_out = refs[len(pieces) + len(spans) :]
        me = lax.axis_index(AXIS)
        loads = []
        for i, (k, q, off) in enumerate(where):
            place = pl.multiple_of((me ^ off) * rows, rows)
            load = pltpu.make_async_copy(
                inputs[k].at[q], held.at[pl.ds(place, rows)], sem_in.at[i]
            )
            load.start()
            loads.append((load, place))
        stores = []
        for i, (load, place) in enumerate(loads):
            load.wait()
            for j, (left, right) in enumerate(spans):
                store = pltpu.make_async_copy(
                    held.at[pl.ds(place, rows), pl.ds(left, right - left)],
                    outputs[j].at[pl.ds(place, rows)],
                    sem_out.at[i, j],
                )
                store.start()
                stores.append(store)
        for store in stores:
            store.wait()

    return pl.pallas_call(
        kernel,
        out_shape=[
            jax.ShapeDtypeStruct((rows * count, right - left), dtype) for left, right in spans
        ],
        in_specs=[pl.BlockSpec(memory_space=pl.ANY)] * len(pieces),
        out_specs=[pl.BlockSpec(memory_space=pl.ANY)] * len(spans),
        scratch_shapes=[
            pltpu.VMEM((rows * count, width), dtype),
            pltpu.SemaphoreType.DMA((count,)),
            pltpu.SemaphoreType.DMA((count, len(spans))),
        ],
        cost_estimate=pl.CostEstimate(
            flops=0, bytes_accessed=4 * rows * count * width, transcendentals=0
        ),
    )(*[b for b, _ in pieces])


def pick(value, axis, index):
    return lax.dynamic_index_in_dim(value, index, axis, keepdims=False)


def joined(blocks, dtype):
    return blocks[0].astype(dtype) if len(blocks) == 1 else jnp.concatenate(
        [b.astype(dtype) for b in blocks], -1
    )


def reduce_core(grads, me, count):
    shaped = [
        g.reshape(count // 8, 2, 2, 2, g.shape[0] // count, g.shape[1]) for g in grads
    ]
    core = me & 1
    away = joined([pick(g, 3, 1 - core) for g in shaped], jnp.bfloat16)
    back = swap(away, CORE, count)
    own = joined([pick(g, 3, core) for g in shaped], jnp.float32)
    return (own + back.astype(jnp.float32)).astype(jnp.bfloat16)


def reduce_pair(part, me, count, *tokens):
    part = after(part, *tokens)
    y, x = (me >> 2) & 1, (me >> 1) & 1
    half = part.shape[0] // 2

    def line(dy, dx):
        return pick(pick(part, 1, y ^ dy), 1, x ^ dx)

    far = line(1, 1)
    low = swap(far[:half], PAIR_X, count)
    high = swap(far[half:], PAIR_Y, count)
    zeros = jnp.zeros_like(low)
    to_y = line(1, 0).astype(jnp.float32) + jnp.concatenate([low, zeros], 0).astype(jnp.float32)
    to_x = line(0, 1).astype(jnp.float32) + jnp.concatenate([zeros, high], 0).astype(jnp.float32)
    from_y = swap(to_y.astype(jnp.bfloat16), PAIR_Y, count)
    from_x = swap(to_x.astype(jnp.bfloat16), PAIR_X, count)
    own = (
        line(0, 0).astype(jnp.float32)
        + from_y.astype(jnp.float32)
        + from_x.astype(jnp.float32)
    )
    return own, (low, high), (from_y, from_x)


def reduce_line(part, me, count, *tokens):
    part = after(part, *tokens)
    rest = part.shape[1:]
    for bit in reversed(line_bits(count)):
        halves = part.reshape(part.shape[0] // 2, 2, *rest)
        mine = (me // bit) & 1
        away = pick(halves, 1, 1 - mine).astype(jnp.bfloat16)
        part = pick(halves, 1, mine) + swap(away, bit, count).astype(jnp.float32)
    return part.reshape(rest)


def layer_norm_apply(value_rows):
    centred = value_rows - jnp.mean(value_rows, -1, keepdims=True)
    spread = jnp.mean(centred * centred, -1, keepdims=True)
    factor = lax.rsqrt(spread + EPS_NORM)
    return (centred * factor, factor)


def norm_backward_pass(scaled, normed, factor):
    first = jnp.mean(scaled, -1, keepdims=True)
    second = jnp.mean(scaled * normed, -1, keepdims=True)
    return factor * (scaled - first - normed * second)


def gelu_tanh(upper_projection):
    inner = GELU_C * (
        upper_projection + GELU_A * upper_projection * upper_projection * upper_projection
    )
    return 0.5 * upper_projection * (1.0 + jnp.tanh(inner))


def gelu_slope(upper_projection):
    inner = GELU_C * (
        upper_projection + GELU_A * upper_projection * upper_projection * upper_projection
    )
    tangent = jnp.tanh(inner)
    return 0.5 * (1.0 + tangent) + 0.5 * upper_projection * (1.0 - tangent * tangent) * GELU_C * (
        1.0 + 3.0 * GELU_A * upper_projection * upper_projection
    )


def inner_rows(left, right, out=jnp.float32):
    return lax.dot_general(
        left, right, (((0,), (0,)), ((), ())), preferred_element_type=jnp.float32
    ).astype(out)


def outer_cols(left, right):
    return lax.dot_general(
        left, right, (((1,), (1,)), ((), ())), preferred_element_type=jnp.float32
    )


def score_terms(q, k, segs):
    micro, length, heads, _ = q.shape
    places = jnp.arange(length, dtype=jnp.int32)
    distance = (places[:, None] - places[None, :]).astype(jnp.float32)
    allowed = (places[:, None] >= places[None, :])[None] & (
        segs[:, :, None] == segs[:, None, :]
    )
    slopes = 2.0 ** (-8.0 * (jnp.arange(heads, dtype=jnp.float32) + 1.0) / heads)
    scores = jnp.einsum("bihd,bjhd->bhij", q, k, preferred_element_type=jnp.float32)
    scores = scores * HEAD_DIM ** (-0.5) - slopes[None, :, None, None] * distance
    return jnp.where(allowed[:, None], scores, -1e30)


def attend(q, k, v, segs):
    scores = score_terms(q, k, segs)
    log_sum_exponent = jnp.log(jnp.sum(jnp.exp(scores), -1))
    probs = jnp.exp(scores - log_sum_exponent[..., None]).astype(jnp.bfloat16)
    attended = jnp.einsum("bhij,bjhd->bihd", probs, v, preferred_element_type=jnp.float32)
    return attended.astype(jnp.bfloat16), log_sum_exponent


def attend_back(q, k, v, attended, log_sum_exponent, d_attended, segs):
    scores = score_terms(q, k, segs)
    probs = jnp.exp(scores - log_sum_exponent[..., None])
    probs_half = probs.astype(jnp.bfloat16)
    delta = jnp.sum(d_attended.astype(jnp.float32) * attended.astype(jnp.float32), -1)
    delta = delta.transpose(0, 2, 1)
    d_values = jnp.einsum(
        "bhij,bihd->bjhd", probs_half, d_attended, preferred_element_type=jnp.float32
    )
    d_probs = jnp.einsum("bihd,bjhd->bhij", d_attended, v, preferred_element_type=jnp.float32)
    d_scores = (probs * (d_probs - delta[..., None]) * HEAD_DIM ** (-0.5)).astype(jnp.bfloat16)
    d_query = jnp.einsum("bhij,bjhd->bihd", d_scores, k, preferred_element_type=jnp.float32)
    d_keys = jnp.einsum("bhij,bihd->bjhd", d_scores, q, preferred_element_type=jnp.float32)
    return d_query, d_keys, d_values


def adamw(weight, grad, moment, square, decay, rate):
    moment_next = 0.9 * moment + 0.1 * grad
    square_next = 0.95 * square + 0.05 * grad * grad
    first = moment_next / (1.0 - 0.9**ADAM_STEP)
    second = square_next / (1.0 - 0.95**ADAM_STEP)
    change = first / (jnp.sqrt(second) + 1e-08) + decay * weight
    return (weight - rate * change, moment_next, square_next)


SMALL = 128


def shards(hidden_in, out_grad, segment_ids, *state):
    masters, moments, squares = state[:7], state[7:14], state[14:]
    count = lax.axis_size(AXIS)
    me = lax.axis_index(AXIS)
    micro, length = segment_ids.shape
    tokens, width = hidden_in.shape
    heads = width // HEAD_DIM
    gains, biases, heads_w, output_w, expand_w, widen_b, shrink_w = (
        item.astype(jnp.bfloat16) for item in masters
    )
    rows = heads_w.shape[0]
    wide = widen_b.shape[0] // rows
    n_gain, n_bias = gains.shape[0], biases.shape[0]
    small = jnp.concatenate([gains.T, biases.T, widen_b.reshape(rows, wide)], 1)
    small = jnp.pad(small, ((0, 0), (0, SMALL - small.shape[1])))

    first = jnp.concatenate([heads_w, output_w, small], 1)
    line_a, offsets = gather_line(first, count)
    line_b, _ = gather_line(expand_w, count, line_a)
    line_c, _ = gather_line(shrink_w, count, line_b)
    got_a = gather_pair(line_a, offsets, count)
    got_b = gather_pair(line_b, offsets, count, got_a[3][0], got_a[4][0])
    got_c = gather_pair(line_c, offsets, count, got_b[3][0], got_b[4][0])
    three = heads_w.shape[1]
    heads_full, output_full, small_full = assemble(
        gather_core(got_a, count), count, (0, three, three + width, three + width + SMALL)
    )
    (expand_full,) = assemble(gather_core(got_b, count), count, (0, expand_w.shape[1]))
    (shrink_full,) = assemble(gather_core(got_c, count), count, (0, width))
    small_full = small_full.astype(jnp.float32)
    gain = small_full[:, :n_gain].T
    bias = small_full[:, n_gain : n_gain + n_bias].T
    widen = small_full[:, n_gain + n_bias : n_gain + n_bias + wide].reshape(-1)

    start = hidden_in.astype(jnp.float32)
    xhat1, factor1 = layer_norm_apply(start)
    normed1 = (xhat1 * gain[0] + bias[0]).astype(jnp.bfloat16)
    mixed = jnp.dot(normed1, heads_full, preferred_element_type=jnp.float32)
    four = (micro, length, heads, HEAD_DIM)
    query = (mixed[:, :width] + bias[1]).astype(jnp.bfloat16).reshape(four)
    keys = mixed[:, width : 2 * width].astype(jnp.bfloat16).reshape(four)
    values = (mixed[:, 2 * width :] + bias[2]).astype(jnp.bfloat16).reshape(four)
    attended4, log_sum = attend(query, keys, values, segment_ids)
    attended = attended4.reshape(tokens, width)
    hidden1 = start + jnp.dot(attended, output_full, preferred_element_type=jnp.float32) + bias[3]
    xhat2, factor2 = layer_norm_apply(hidden1)
    normed2 = (xhat2 * gain[1] + bias[4]).astype(jnp.bfloat16)
    upper = jnp.dot(normed2, expand_full, preferred_element_type=jnp.float32) + widen
    active = gelu_tanh(upper).astype(jnp.bfloat16)

    dy = out_grad.astype(jnp.float32)
    g_shrink = inner_rows(active, out_grad, jnp.bfloat16)
    core_s = reduce_core([g_shrink], me, count)
    pair_s, far_s, near_s = reduce_pair(core_s, me, count, got_c[3][0], got_c[4][0])
    sum_s = reduce_line(pair_s, me, count)

    block_out = (
        hidden1 + jnp.dot(active, shrink_full, preferred_element_type=jnp.float32) + bias[5]
    ).astype(jnp.bfloat16)
    d_upper = outer_cols(out_grad, shrink_full) * gelu_slope(upper)
    d_upper_half = d_upper.astype(jnp.bfloat16)
    g_expand = inner_rows(normed2, d_upper_half, jnp.bfloat16)
    core_e = reduce_core([g_expand], me, count)
    pair_e, far_e, near_e = reduce_pair(core_e, me, count, *near_s)
    sum_e = reduce_line(pair_e, me, count)

    d_normed2 = outer_cols(d_upper_half, expand_full)
    d_hidden1 = dy + norm_backward_pass(d_normed2 * gain[1], xhat2, factor2)
    d_hidden1_half = d_hidden1.astype(jnp.bfloat16)
    g_output = inner_rows(attended, d_hidden1_half, jnp.bfloat16)
    d_attended = outer_cols(d_hidden1_half, output_full).astype(jnp.bfloat16).reshape(four)
    d_query, d_keys, d_values = (
        item.reshape(tokens, width)
        for item in attend_back(
            query, keys, values, attended4, log_sum, d_attended, segment_ids
        )
    )
    d_mixed = jnp.concatenate([d_query, d_keys, d_values], 1).astype(jnp.bfloat16)
    g_heads = inner_rows(normed1, d_mixed, jnp.bfloat16)
    d_normed1 = outer_cols(d_mixed, heads_full)
    input_gradient = d_hidden1 + norm_backward_pass(d_normed1 * gain[0], xhat1, factor1)

    g_small = jnp.stack(
        [
            jnp.sum(d_normed1 * xhat1, 0),
            jnp.sum(d_normed2 * xhat2, 0),
            jnp.sum(d_normed1, 0),
            jnp.sum(d_query, 0),
            jnp.sum(d_values, 0),
            jnp.sum(d_hidden1, 0),
            jnp.sum(d_normed2, 0),
            jnp.sum(dy, 0),
        ],
        1,
    )
    g_small = jnp.concatenate([g_small, jnp.sum(d_upper, 0).reshape(-1, wide)], 1)
    g_small = jnp.pad(g_small, ((0, 0), (0, SMALL - g_small.shape[1])))
    core_h = reduce_core([g_heads, g_output, g_small], me, count)
    pair_h, far_h, near_h = reduce_pair(core_h, me, count, *near_e)
    sum_h = reduce_line(pair_h, me, count)

    tail = sum_h[:, three + width :]
    totals = (
        tail[:, :n_gain].T,
        tail[:, n_gain : n_gain + n_bias].T,
        sum_h[:, :three],
        sum_h[:, three : three + width],
        sum_e,
        tail[:, n_gain + n_bias : n_gain + n_bias + wide].reshape(-1),
        sum_s,
    )
    steps = [
        adamw(*item)
        for item in zip(masters, totals, moments, squares, DECAYS, LEARN_RATES)
    ]
    updated, momenta, variances = zip(*steps)
    return (block_out, input_gradient, *totals, *updated, *momenta, *variances)


def solution(mesh):
    rows, cols, flat = P(AXIS, None), P(None, AXIS), P(AXIS)
    params = (cols, cols, rows, rows, rows, flat, rows)
    return jax.shard_map(
        shards,
        mesh=mesh,
        in_specs=(rows, rows, rows) + params * 3,
        out_specs=(rows, rows) + params * 4,
        check_vma=False,
    )
```
